32 devices in a mesh: parts: 2 (over y), row: 8 (over z, x), col: 2 (over core).
Axes of the slice: x: 2, y: 2, z: 4, core: 2. Of those that a mesh axis runs over, the one named last changes fastest.
Arguments:
- queries: bfloat16 [16384, 256], P(('parts', 'row', 'col')), parts along dimension 0, may hold values from -6 to 6
- counts: int32 [32], P(('parts', 'row', 'col')), parts along dimension 0, may hold values from 1 to 512, as said below
- memory: bfloat16 [512, 256], P(('parts', 'row', 'col')), parts along dimension 0, may hold values from -6 to 6
- mem_mask: int32 [512], P(('parts', 'row', 'col')), parts along dimension 0, may hold values from 0 to 1, as said below
- cross_wq: bfloat16 [256, 256], replicated, may hold values from -0.375 to 0.375
- cross_wkv: bfloat16 [256, 512], replicated, may hold values from -0.375 to 0.375
- cross_wo: bfloat16 [256, 256], replicated, may hold values from -0.375 to 0.375
- self_wqkv: bfloat16 [256, 768], replicated, may hold values from -0.375 to 0.375
- self_wo: bfloat16 [256, 256], replicated, may hold values from -0.375 to 0.375
- ffn_up: bfloat16 [256, 2048], replicated, may hold values from -0.375 to 0.375
- ffn_down: bfloat16 [2048, 256], replicated, may hold values from -0.125 to 0.125
- box_w1: bfloat16 [256, 256], replicated, may hold values from -0.375 to 0.375
- box_w2: bfloat16 [256, 256], replicated, may hold values from -0.375 to 0.375
- box_w3: bfloat16 [256, 4], replicated, may hold values from -0.375 to 0.375
- cross_temp: float32 [8], replicated, may hold values from 1 to 100
- self_temp: float32 [8], replicated, may hold values from 1 to 100
Outputs:
- features: float32 [16384, 256], P(('parts', 'row', 'col')), parts along dimension 0
- boxes: float32 [4, 16384], P(None, ('parts', 'row', 'col')), parts along dimension 1
The draws below stay inside these ranges and needn't reach their ends.
There are 2 independent parts, one for each index of `parts`. The reference program is written for one: setup_inputs(seed, part) draws one part's arguments, and reference() takes and returns one part's arrays. A program takes and returns all parts, laid end to end along the dimension named above; an argument that names none is the same for every part. Nothing has to cross between parts.
Inputs may be any that keep to these rules, and one draw needn't show every extreme that they name: The first counts[t] slots of tile t are live; some tile is full. `mem_mask`: the first memory token of every tile is live.
All inputs are finite; a program needn't handle non-finite values.
Results may differ from the reference program's by a relative error of at most 0.038.
The reference program's roundings to bfloat16 on the way (of `qc`, `kvm`, `ctx`, `qkv`, `sctx`, `upper` and `b2`) count: a program that leaves them out, or rounds other values in their place, can miss the bound.
Values may be sent and summed in bfloat16 or wider, within the bound.
A program may use at most 64 MiB of HBM per device.

```python
import math
import jax
import jax.numpy as jnp
from jax import lax

D = 256
HEADS = 8
FF = 2048
Q_DEV = 512
M_DEV = 16
TILES = 16
NQ = 8192
MEM = 256
N_ROW = 8
N_COL = 2


def draw_counts(key, part):
    first = jax.random.fold_in(key, 11)
    second = jax.random.fold_in(key, 12)
    values = jax.random.randint(first, (TILES,), 1, Q_DEV + 1)
    full_tile = jax.random.randint(second, (), 0, TILES)
    return jnp.where(jnp.arange(TILES) == full_tile, Q_DEV, values).astype(jnp.int32)


def draw_mem_mask(key, part):
    bits = jax.random.randint(jax.random.fold_in(key, 21), (MEM,), 0, 4)
    first = jnp.arange(MEM) % M_DEV == 0
    return jnp.where((bits > 0) | first, 1, 0).astype(jnp.int32)


def temper(key, salt):
    spread = jax.random.uniform(jax.random.fold_in(key, salt), (HEADS,), jnp.float32)
    high = jnp.full((HEADS,), math.log(6.0), jnp.float32)
    return jnp.exp(spread * high).astype(jnp.float32)


def draw_cross_temp(key, part):
    return temper(key, 31)


def draw_self_temp(key, part):
    return temper(key, 41)


def level_of(own_key, shape, cuts, low, top_value):
    def one(position, parts):
        heights = jax.random.uniform(jax.random.fold_in(jax.random.fold_in(own_key, 6), position), (parts,), jnp.float32, low / len(cuts), top_value / len(cuts))
        return jnp.repeat(jnp.exp(heights), shape[position] // parts).reshape((-1,) + (1,) * (len(shape) - position - 1))

    gain = one(*cuts[0])
    for cut in cuts[1:]:
        gain = gain * one(*cut)
    return gain


def bell_draw(own_key, dims, scale, limit, pieces=(), held_as=jnp.bfloat16):
    array = jax.random.normal(own_key, dims, jnp.float32) * scale
    if len(pieces) > 0:
        array = level_of(own_key, dims, pieces, -0.22, 0.18) * array
    return jnp.clip(array, min=-limit, max=limit).astype(held_as)


def setup_inputs(seed: int = 0, part: int = 0) -> dict:
    splits = jax.random.split(jax.random.key(seed), 17)
    part_splits = jax.random.split(jax.random.fold_in(splits[16], part), 17)
    queries = bell_draw(part_splits[0], (NQ, D), 1.0, 6.0, ((0, 16),))
    counts = draw_counts(jax.random.fold_in(jax.random.fold_in(splits[16], part), 71), part)
    memory = bell_draw(part_splits[2], (MEM, D), 1.0, 6.0, ((0, 16),))
    mem_mask = draw_mem_mask(jax.random.fold_in(jax.random.fold_in(splits[16], part), 71), part)
    cross_wq = bell_draw(splits[4], (D, D), D ** -0.5, 0.375)
    cross_wkv = bell_draw(splits[5], (D, 2 * D), D ** -0.5, 0.375)
    cross_wo = bell_draw(splits[6], (D, D), D ** -0.5, 0.375)
    self_wqkv = bell_draw(splits[7], (D, 3 * D), D ** -0.5, 0.375)
    self_wo = bell_draw(splits[8], (D, D), D ** -0.5, 0.375)
    ffn_up = bell_draw(splits[9], (D, FF), D ** -0.5, 0.375)
    ffn_down = bell_draw(splits[10], (FF, D), FF ** -0.5, 0.125)
    box_w1 = bell_draw(splits[11], (D, D), D ** -0.5, 0.375)
    box_w2 = bell_draw(splits[12], (D, D), D ** -0.5, 0.375)
    box_w3 = bell_draw(splits[13], (D, 4), D ** -0.5, 0.375)
    cross_temp = draw_cross_temp(jax.random.fold_in(splits[16], 71), part)
    self_temp = draw_self_temp(jax.random.fold_in(splits[16], 71), part)
    return dict(queries=queries, counts=counts, memory=memory, mem_mask=mem_mask, cross_wq=cross_wq, cross_wkv=cross_wkv, cross_wo=cross_wo, self_wqkv=self_wqkv, self_wo=self_wo, ffn_up=ffn_up, ffn_down=ffn_down, box_w1=box_w1, box_w2=box_w2, box_w3=box_w3, cross_temp=cross_temp, self_temp=self_temp)


EPS = 1e-06

def rms_norm(x):
    return x * lax.rsqrt(lax.optimization_barrier(jnp.mean(x * x, axis=-1, keepdims=True)) + EPS)

def attend(query, keyval, live, scale):
    rows = query.shape[0]
    width = query.shape[1]
    heads = scale.shape[0]
    hsize = width // heads
    q3 = query.astype(jnp.float32).reshape(rows, heads, hsize)
    keys = keyval[:, :width].astype(jnp.float32).reshape(-1, heads, hsize)
    values = keyval[:, width:].astype(jnp.float32).reshape(-1, heads, hsize)
    scores = jnp.einsum('qhd,khd->hqk', q3, keys, precision=lax.Precision.HIGHEST) * scale[:, None, None]
    keep = (live > 0)[None, None, :]
    top = lax.optimization_barrier(jnp.max(jnp.where(keep, scores, -1e+30), axis=-1, keepdims=True))
    weights = jnp.where(keep, jnp.exp(scores - top), 0.0)
    total = lax.optimization_barrier(jnp.sum(weights, axis=-1))
    rounded = lax.optimization_barrier(weights.astype(jnp.bfloat16)).astype(jnp.float32)
    mixed = jnp.einsum('hqk,khd->qhd', rounded, values, precision=lax.Precision.HIGHEST)
    mixed = mixed / jnp.transpose(total)[:, :, None]
    return mixed.reshape(rows, width)

def reference(queries, counts, memory, mem_mask, cross_wq, cross_wkv, cross_wo, self_wqkv, self_wo, ffn_up, ffn_down, box_w1, box_w2, box_w3, cross_temp, self_temp):
    hsize = D // HEADS
    slots = jnp.arange(Q_DEV, dtype=jnp.int32)
    valid = (slots[None, :] < counts[:, None]).reshape(NQ)
    xres = queries.astype(jnp.float32)
    hn0 = rms_norm(xres).astype(jnp.bfloat16)
    qc = jnp.dot(hn0, cross_wq, preferred_element_type=jnp.float32).astype(jnp.bfloat16)
    kvm = jnp.dot(memory, cross_wkv, preferred_element_type=jnp.float32).astype(jnp.bfloat16)
    scale_c = cross_temp / jnp.sqrt(jnp.float32(hsize))
    q_tiles = qc.reshape(N_ROW, N_COL, Q_DEV, D)
    kv_tiles = kvm.reshape(N_ROW, N_COL, M_DEV, 2 * D)
    m_tiles = mem_mask.reshape(N_ROW, N_COL, M_DEV)
    columns = []
    for column in range(N_COL):
        strip = kv_tiles[:, column].reshape(N_ROW * M_DEV, 2 * D)
        strip_live = m_tiles[:, column].reshape(N_ROW * M_DEV)
        columns.append(lax.map(lambda q: attend(q, strip, strip_live, scale_c), q_tiles[:, column]))
    ctx = jnp.stack(columns, axis=1).reshape(NQ, D)
    ctx = jnp.where(valid[:, None], ctx, 0.0).astype(jnp.bfloat16)
    x1 = xres + jnp.dot(ctx, cross_wo, preferred_element_type=jnp.float32)
    hn1 = rms_norm(x1).astype(jnp.bfloat16)
    qkv = jnp.dot(hn1, self_wqkv, preferred_element_type=jnp.float32).astype(jnp.bfloat16)
    scale_s = self_temp / jnp.sqrt(jnp.float32(hsize))
    row_qkv = qkv.reshape(N_ROW, N_COL * Q_DEV, 3 * D)
    row_live = valid.astype(jnp.int32).reshape(N_ROW, N_COL * Q_DEV)

    def self_row(pair):
        block, live = pair
        return attend(block[:, :D], block[:, D:], live, scale_s)
    sctx = lax.map(self_row, (row_qkv, row_live)).reshape(NQ, D)
    sctx = jnp.where(valid[:, None], sctx, 0.0).astype(jnp.bfloat16)
    x2 = x1 + jnp.dot(sctx, self_wo, preferred_element_type=jnp.float32)
    hn2 = rms_norm(x2).astype(jnp.bfloat16)
    upper = jnp.maximum(jnp.dot(hn2, ffn_up, preferred_element_type=jnp.float32), 0.0).astype(jnp.bfloat16)
    x3 = x2 + jnp.dot(upper, ffn_down, preferred_element_type=jnp.float32)
    features = jnp.where(valid[:, None], x3, 0.0).astype(jnp.float32)
    hn3 = rms_norm(x3).astype(jnp.bfloat16)
    b1 = jnp.maximum(jnp.dot(hn3, box_w1, preferred_element_type=jnp.float32), 0.0).astype(jnp.bfloat16)
    b2 = jnp.maximum(jnp.dot(b1, box_w2, preferred_element_type=jnp.float32), 0.0).astype(jnp.bfloat16)
    raw_box = jax.nn.sigmoid(jnp.dot(b2, box_w3, preferred_element_type=jnp.float32))
    boxes = jnp.transpose(jnp.where(valid[:, None], raw_box, 0.0))
    return (features, boxes)
```

```python
import functools
import math

import jax
import jax.numpy as jnp
from jax import lax
from jax.experimental import pallas as pl
from jax.experimental.pallas import tpu as pltpu
from jax.sharding import PartitionSpec as P

EPS = 1e-06
LANES = 128
BF = jnp.bfloat16
F32 = jnp.float32
MESH = pl.DeviceIdType.MESH


def rms_round(x):
    return (x * lax.rsqrt(jnp.mean(x * x, axis=-1, keepdims=True) + EPS)).astype(BF)


def mm(a, b):
    return jnp.dot(a, b, preferred_element_type=F32)


def each(n, body):
    if n <= 16:
        for i in range(n):
            body(i)
    else:
        lax.fori_loop(0, n, lambda i, c: (body(i), c)[1], 0)


def scale_row(temp_ref, width, hsize):
    head = lax.broadcasted_iota(jnp.int32, (1, width), 1) // hsize
    row = jnp.zeros((1, width), F32)
    for h in range(width // hsize):
        row = jnp.where(head == h, temp_ref[h], row)
    return row * (math.log2(math.e) / math.sqrt(hsize))


def attend(q, row, ka_ref, va_ref, hsize):
    rows, width = q.shape
    per = LANES // hsize
    qf = q.astype(F32) * row
    hi = qf.astype(BF).astype(F32)
    lo = qf - hi
    head = lax.broadcasted_iota(jnp.int32, (rows, LANES), 1) // hsize
    outs = []
    for g in range(width // LANES):
        lanes = slice(g * LANES, (g + 1) * LANES)
        lhs = jnp.concatenate(
            [
                jnp.concatenate(
                    [jnp.where(head == h, hi[:, lanes], 0.0), jnp.where(head == h, lo[:, lanes], 0.0)],
                    axis=1,
                ).astype(BF)
                for h in range(per)
            ],
            axis=0,
        )
        s = lax.dot_general(lhs, ka_ref[g], (((1,), (1,)), ((), ())), preferred_element_type=F32)
        e = jnp.exp2(s - jnp.max(s, axis=-1, keepdims=True)).astype(BF)
        o = mm(e, va_ref[g])
        num, den = o[:rows, :LANES], o[:rows, LANES:]
        for h in range(1, per):
            part = o[h * rows : (h + 1) * rows]
            num = jnp.where(head == h, part[:, :LANES], num)
            den = jnp.where(head == h, part[:, LANES:], den)
        outs.append(num / den)
    return jnp.concatenate(outs, axis=1)


def put_keys(ka_ref, va_ref, rows, k, v, live, first):
    flags = live.astype(F32).astype(BF)
    for g in range(k.shape[1] // LANES):
        lanes = slice(g * LANES, (g + 1) * LANES)
        kg = jnp.where(live, k[:, lanes], first[:, lanes]).astype(BF)
        ka_ref[g, rows, :LANES] = kg
        ka_ref[g, rows, LANES:] = kg
        va_ref[g, rows, :LANES] = jnp.where(live, v[:, lanes], 0.0).astype(BF)
        va_ref[g, rows, LANES:] = flags


def kernel(
    n_row, hsize, tm,
    q_hbm, cnt_s, mem_hbm, mask_s, wq_h, wkv_h, wo_h, wqkv_h, swo_h, up_h, down_h, w1_h, w2_h, w3_h,
    ct_s, st_s,
    feat_ref, box_ref,
    q_v, wq, wkv, wo, wqkv, swo, up, down, w1, w2, w3,
    gat, cnt, kac, vac, kas, vas, qc_v, x1_v, hn_v, hn_o, qs_v, sc_v,
    in_sem, gsend, grecv, csend, crecv, hsend, hrecv, msem,
):
    n, width = q_v.shape
    m_dev = mem_hbm.shape[0]
    row = lax.axis_index("row")
    other = 1 - lax.axis_index("col")

    barrier = pltpu.get_barrier_semaphore()

    def greet(i):
        pl.semaphore_signal(
            barrier, inc=1, device_id={"row": lax.rem(row + 1 + i, n_row)}, device_id_type=MESH
        )

    each(n_row - 1, greet)
    pl.semaphore_signal(barrier, inc=1, device_id={"col": other}, device_id_type=MESH)

    mine = pltpu.make_async_copy(mem_hbm, gat.at[row, :, pl.ds(0, width)], msem)
    mine.start()
    pairs = (
        (q_hbm, q_v), (wq_h, wq), (wkv_h, wkv), (wo_h, wo), (wqkv_h, wqkv),
        (swo_h, swo), (up_h, up), (down_h, down), (w1_h, w1), (w2_h, w2), (w3_h, w3),
    )
    loads = [pltpu.make_async_copy(a, b, in_sem.at[i]) for i, (a, b) in enumerate(pairs)]
    for load in loads:
        load.start()

    slot = lax.broadcasted_iota(jnp.int32, (m_dev, LANES), 0)
    flags = jnp.zeros((m_dev, LANES), jnp.int32)
    for i in range(m_dev):
        flags = jnp.where(slot == i, mask_s[i], flags)
    gat[row, :, pl.ds(width, LANES)] = (flags > 0).astype(F32).astype(BF)
    count = cnt_s[0]
    cnt[0] = jnp.full((8, LANES), count, jnp.int32)
    mine.wait()
    pl.semaphore_wait(barrier, n_row)

    def gather_copy(i):
        return pltpu.make_async_remote_copy(
            src_ref=gat.at[row], dst_ref=gat.at[row],
            send_sem=gsend.at[i], recv_sem=grecv.at[row],
            device_id={"row": lax.rem(row + 1 + i, n_row)}, device_id_type=MESH,
        )

    each(n_row - 1, lambda i: gather_copy(i).start())
    count_copy = pltpu.make_async_remote_copy(
        src_ref=cnt.at[0], dst_ref=cnt.at[1], send_sem=csend, recv_sem=crecv,
        device_id={"col": other}, device_id_type=MESH,
    )
    count_copy.start()

    loads[0].wait()
    loads[1].wait()
    qc_v[...] = mm(rms_round(q_v[...].astype(F32)), wq[...]).astype(BF)
    loads[2].wait()

    def arrived(i):
        j = lax.rem(row + 1 + i, n_row)
        pltpu.make_async_remote_copy(
            src_ref=gat.at[j], dst_ref=gat.at[j],
            send_sem=gsend.at[i], recv_sem=grecv.at[j],
            device_id={"row": j}, device_id_type=MESH,
        ).wait_recv()

    each(n_row - 1, arrived)

    keys = n_row * m_dev
    held = gat[...].reshape(keys, width + LANES)
    kv = mm(held[:, :width], wkv[...])
    live = held[:, width:].astype(F32) > 0.0
    put_keys(kac, vac, pl.ds(0, keys), kv[:, :width], kv[:, width:], live, kv[0:1, :width])

    cross_row = scale_row(ct_s, width, hsize)
    loads[3].wait()

    def hn_copy(t):
        rows = pl.ds(pl.multiple_of(t * tm, tm), tm)
        return pltpu.make_async_remote_copy(
            src_ref=hn_v.at[rows], dst_ref=hn_o.at[rows],
            send_sem=hsend.at[t], recv_sem=hrecv.at[t],
            device_id={"col": other}, device_id_type=MESH,
        )

    def cross_tile(t, carry):
        rows = pl.ds(pl.multiple_of(t * tm, tm), tm)
        ctx = attend(qc_v[rows, :], cross_row, kac, vac, hsize)
        alive = lax.broadcasted_iota(jnp.int32, (tm, width), 0) + t * tm < count
        ctx = jnp.where(alive, ctx, 0.0).astype(BF)
        x1 = q_v[rows, :].astype(F32) + mm(ctx, wo[...])
        x1_v[rows, :] = x1
        hn_v[rows, :] = rms_round(x1)
        hn_copy(t).start()
        return carry

    lax.fori_loop(0, n // tm, cross_tile, 0)

    loads[4].wait()
    qkv = mm(hn_v[...], wqkv[...])
    qs_v[...] = qkv[:, :width].astype(BF)
    k = qkv[:, width : 2 * width]
    first = k[0:1]
    spot = lax.broadcasted_iota(jnp.int32, (n, LANES), 0)
    put_keys(kas, vas, pl.ds(0, n), k, qkv[:, 2 * width :], spot < count, first)
    count_copy.wait()
    each(n // tm, lambda t: hn_copy(t).wait())
    kv_o = mm(hn_o[...], wqkv[:, width:])
    put_keys(kas, vas, pl.ds(n, n), kv_o[:, :width], kv_o[:, width:], spot < cnt[1, 0:1, :], first)

    self_row = scale_row(st_s, width, hsize)

    def self_tile(t, carry):
        rows = pl.ds(pl.multiple_of(t * tm, tm), tm)
        sctx = attend(qs_v[rows, :], self_row, kas, vas, hsize)
        alive = lax.broadcasted_iota(jnp.int32, (tm, width), 0) + t * tm < count
        sc_v[rows, :] = jnp.where(alive, sctx, 0.0).astype(BF)
        return carry

    lax.fori_loop(0, n // tm, self_tile, 0)

    for load in loads[5:]:
        load.wait()
    x2 = x1_v[...] + mm(sc_v[...], swo[...])
    hn2 = rms_round(x2)
    ff = up.shape[1]
    step = min(512, ff)
    x3 = x2
    for f in range(0, ff, step):
        upper = jnp.maximum(mm(hn2, up[:, f : f + step]), 0.0).astype(BF)
        x3 = x3 + mm(upper, down[f : f + step, :])
    alive = lax.broadcasted_iota(jnp.int32, (n, width), 0) < count
    feat_ref[...] = jnp.where(alive, x3, 0.0)
    hn3 = rms_round(x3)
    b1 = jnp.maximum(mm(hn3, w1[...]), 0.0).astype(BF)
    b2 = jnp.maximum(mm(b1, w2[...]), 0.0).astype(BF)
    z = lax.dot_general(w3[...], b2, (((0,), (1,)), ((), ())), preferred_element_type=F32)
    box = 1.0 / (1.0 + jnp.exp(-z))
    box_ref[...] = jnp.where(lax.broadcasted_iota(jnp.int32, box.shape, 1) < count, box, 0.0)

    each(n_row - 1, lambda i: gather_copy(i).wait_send())


def local(n_row, *args):
    queries, counts, memory, mem_mask = args[:4]
    weights = args[4:14]
    n, width = queries.shape
    m_dev = memory.shape[0]
    heads = args[14].shape[0]
    keys = n_row * m_dev
    groups = width // LANES
    tm = min(128, n)
    smem = pl.BlockSpec(memory_space=pltpu.SMEM)
    anyw = pl.BlockSpec(memory_space=pl.ANY)
    vmem = pl.BlockSpec(memory_space=pltpu.VMEM)
    dma = pltpu.SemaphoreType.DMA
    boxes = weights[-1].shape[1]
    return pl.pallas_call(
        functools.partial(kernel, n_row, width // heads, tm),
        out_shape=(
            jax.ShapeDtypeStruct((n, width), F32),
            jax.ShapeDtypeStruct((boxes, n), F32),
        ),
        in_specs=[anyw, smem, anyw, smem] + [anyw] * 10 + [smem, smem],
        out_specs=(vmem, vmem),
        scratch_shapes=[pltpu.VMEM(queries.shape, BF)]
        + [pltpu.VMEM(w.shape, BF) for w in weights]
        + [
            pltpu.VMEM((n_row, m_dev, width + LANES), BF),
            pltpu.VMEM((2, 8, LANES), jnp.int32),
            pltpu.VMEM((groups, keys, 2 * LANES), BF),
            pltpu.VMEM((groups, keys, 2 * LANES), BF),
            pltpu.VMEM((groups, 2 * n, 2 * LANES), BF),
            pltpu.VMEM((groups, 2 * n, 2 * LANES), BF),
            pltpu.VMEM((n, width), BF),
            pltpu.VMEM((n, width), F32),
            pltpu.VMEM((n, width), BF),
            pltpu.VMEM((n, width), BF),
            pltpu.VMEM((n, width), BF),
            pltpu.VMEM((n, width), BF),
            dma((11,)),
            dma((n_row - 1,)),
            dma((n_row,)),
            dma,
            dma,
            dma((n // tm,)),
            dma((n // tm,)),
            dma,
        ],
        compiler_params=pltpu.CompilerParams(
            collective_id=0, has_side_effects=True, vmem_limit_bytes=52 * 1024 * 1024
        ),
        name="spotter",
    )(*args)


def solution(mesh):
    spread = ("parts", "row", "col")
    return jax.shard_map(
        functools.partial(local, mesh.shape["row"]),
        mesh=mesh,
        in_specs=(P(spread, None), P(spread), P(spread, None), P(spread)) + (P(),) * 12,
        out_specs=(P(spread, None), P(None, spread)),
        check_vma=False,
    )
```

```python
import functools
import math

import jax
import jax.numpy as jnp
from jax import lax
from jax.experimental import pallas as pl
from jax.experimental.pallas import tpu as pltpu
from jax.sharding import PartitionSpec as P

EPS = 1e-06
LANES = 128
BF = jnp.bfloat16
F32 = jnp.float32
MESH = pl.DeviceIdType.MESH


def rms_round(x):
    return (x * lax.rsqrt(jnp.mean(x * x, axis=-1, keepdims=True) + EPS)).astype(BF)


def mm(a, b):
    return jnp.dot(a, b, preferred_element_type=F32)


def each(n, body):
    if n <= 16:
        for i in range(n):
            body(i)
    else:
        lax.fori_loop(0, n, lambda i, c: (body(i), c)[1], 0)


def scale_row(temp_ref, width, hsize):
    head = lax.broadcasted_iota(jnp.int32, (1, width), 1) // hsize
    row = jnp.zeros((1, width), F32)
    for h in range(width // hsize):
        row = jnp.where(head == h, temp_ref[h], row)
    return row * (math.log2(math.e) / math.sqrt(hsize))


def attend(q, row, ka_ref, va_ref, hsize):
    rows, width = q.shape
    per = LANES // hsize
    qf = q.astype(F32) * row
    hi = qf.astype(BF).astype(F32)
    lo = qf - hi
    head = lax.broadcasted_iota(jnp.int32, (rows, LANES), 1) // hsize
    outs = []
    for g in range(width // LANES):
        lanes = slice(g * LANES, (g + 1) * LANES)
        lhs = jnp.concatenate(
            [
                jnp.concatenate(
                    [jnp.where(head == h, hi[:, lanes], 0.0), jnp.where(head == h, lo[:, lanes], 0.0)],
                    axis=1,
                ).astype(BF)
                for h in range(per)
            ],
            axis=0,
        )
        s = lax.dot_general(lhs, ka_ref[g], (((1,), (1,)), ((), ())), preferred_element_type=F32)
        e = jnp.exp2(s - jnp.max(s, axis=-1, keepdims=True)).astype(BF)
        o = mm(e, va_ref[g])
        num, den = o[:rows, :LANES], o[:rows, LANES:]
        for h in range(1, per):
            part = o[h * rows : (h + 1) * rows]
            num = jnp.where(head == h, part[:, :LANES], num)
            den = jnp.where(head == h, part[:, LANES:], den)
        outs.append(num / den)
    return jnp.concatenate(outs, axis=1)


def put_keys(ka_ref, va_ref, rows, k, v, live, first):
    flags = live.astype(F32).astype(BF)
    for g in range(k.shape[1] // LANES):
        lanes = slice(g * LANES, (g + 1) * LANES)
        kg = jnp.where(live, k[:, lanes], first[:, lanes]).astype(BF)
        ka_ref[g, rows, :LANES] = kg
        ka_ref[g, rows, LANES:] = kg
        va_ref[g, rows, :LANES] = jnp.where(live, v[:, lanes], 0.0).astype(BF)
        va_ref[g, rows, LANES:] = flags


def kernel(
    n_row, hsize, tm,
    q_hbm, cnt_s, mem_hbm, mask_s, wq_h, wkv_h, wo_h, wqkv_h, swo_h, up_h, down_h, w1_h, w2_h, w3_h,
    ct_s, st_s,
    feat_ref, box_ref,
    q_v, wq, wkv, wo, wqkv, swo, up, down, w1, w2, w3,
    gat, cnt, kac, vac, kas, vas, qc_v, x1_v, hn_v, hn_o, qs_v, sc_v,
    in_sem, gsend, grecv, csend, crecv, hsend, hrecv, msem,
):
    n, width = q_v.shape
    m_dev = mem_hbm.shape[0]
    row = lax.axis_index("row")
    other = 1 - lax.axis_index("col")

    barrier = pltpu.get_barrier_semaphore()

    def greet(i):
        pl.semaphore_signal(
            barrier, inc=1, device_id={"row": lax.rem(row + 1 + i, n_row)}, device_id_type=MESH
        )

    each(n_row - 1, greet)
    pl.semaphore_signal(barrier, inc=1, device_id={"col": other}, device_id_type=MESH)

    mine = pltpu.make_async_copy(mem_hbm, gat.at[row, :, pl.ds(0, width)], msem)
    mine.start()
    pairs = (
        (q_hbm, q_v), (wq_h, wq), (wkv_h, wkv), (wo_h, wo), (wqkv_h, wqkv),
        (swo_h, swo), (up_h, up), (down_h, down), (w1_h, w1), (w2_h, w2), (w3_h, w3),
    )
    loads = [pltpu.make_async_copy(a, b, in_sem.at[i]) for i, (a, b) in enumerate(pairs)]
    for load in loads:
        load.start()

    slot = lax.broadcasted_iota(jnp.int32, (m_dev, LANES), 0)
    flags = jnp.zeros((m_dev, LANES), jnp.int32)
    for i in range(m_dev):
        flags = jnp.where(slot == i, mask_s[i], flags)
    gat[row, :, pl.ds(width, LANES)] = (flags > 0).astype(F32).astype(BF)
    count = cnt_s[0]
    cnt[0] = jnp.full((8, LANES), count, jnp.int32)
    mine.wait()
    pl.semaphore_wait(barrier, n_row)

    def gather_copy(i):
        return pltpu.make_async_remote_copy(
            src_ref=gat.at[row], dst_ref=gat.at[row],
            send_sem=gsend.at[i], recv_sem=grecv.at[row],
            device_id={"row": lax.rem(row + 1 + i, n_row)}, device_id_type=MESH,
        )

    each(n_row - 1, lambda i: gather_copy(i).start())
    count_copy = pltpu.make_async_remote_copy(
        src_ref=cnt.at[0], dst_ref=cnt.at[1], send_sem=csend, recv_sem=crecv,
        device_id={"col": other}, device_id_type=MESH,
    )
    count_copy.start()

    loads[0].wait()
    loads[1].wait()
    qc_v[...] = mm(rms_round(q_v[...].astype(F32)), wq[...]).astype(BF)
    loads[2].wait()

    def arrived(i):
        j = lax.rem(row + 1 + i, n_row)
        pltpu.make_async_remote_copy(
            src_ref=gat.at[j], dst_ref=gat.at[j],
            send_sem=gsend.at[i], recv_sem=grecv.at[j],
            device_id={"row": j}, device_id_type=MESH,
        ).wait_recv()

    each(n_row - 1, arrived)

    keys = n_row * m_dev
    held = gat[...].reshape(keys, width + LANES)
    kv = mm(held[:, :width], wkv[...])
    live = held[:, width:].astype(F32) > 0.0
    put_keys(kac, vac, pl.ds(0, keys), kv[:, :width], kv[:, width:], live, kv[0:1, :width])

    cross_row = scale_row(ct_s, width, hsize)
    loads[3].wait()

    def hn_copy(t):
        rows = pl.ds(pl.multiple_of(t * tm, tm), tm)
        return pltpu.make_async_remote_copy(
            src_ref=hn_v.at[rows], dst_ref=hn_o.at[rows],
            send_sem=hsend.at[t], recv_sem=hrecv.at[t],
            device_id={"col": other}, device_id_type=MESH,
        )

    def cross_tile(t, carry):
        rows = pl.ds(pl.multiple_of(t * tm, tm), tm)
        ctx = attend(qc_v[rows, :], cross_row, kac, vac, hsize)
        alive = lax.broadcasted_iota(jnp.int32, (tm, width), 0) + t * tm < count
        ctx = jnp.where(alive, ctx, 0.0).astype(BF)
        x1 = q_v[rows, :].astype(F32) + mm(ctx, wo[...])
        x1_v[rows, :] = x1
        hn_v[rows, :] = rms_round(x1)
        hn_copy(t).start()
        return carry

    lax.fori_loop(0, n // tm, cross_tile, 0)

    loads[4].wait()
    qkv = mm(hn_v[...], wqkv[...])
    qs_v[...] = qkv[:, :width].astype(BF)
    k = qkv[:, width : 2 * width]
    first = k[0:1]
    spot = lax.broadcasted_iota(jnp.int32, (n, LANES), 0)
    put_keys(kas, vas, pl.ds(0, n), k, qkv[:, 2 * width :], spot < count, first)
    count_copy.wait()
    each(n // tm, lambda t: hn_copy(t).wait())
    kv_o = mm(hn_o[...], wqkv[:, width:])
    put_keys(kas, vas, pl.ds(n, n), kv_o[:, :width], kv_o[:, width:], spot < cnt[1, 0:1, :], first)

    self_row = scale_row(st_s, width, hsize)

    def self_tile(t, carry):
        rows = pl.ds(pl.multiple_of(t * tm, tm), tm)
        sctx = attend(qs_v[rows, :], self_row, kas, vas, hsize)
        alive = lax.broadcasted_iota(jnp.int32, (tm, width), 0) + t * tm < count
        sc_v[rows, :] = jnp.where(alive, sctx, 0.0).astype(BF)
        return carry

    lax.fori_loop(0, n // tm, self_tile, 0)

    for load in loads[5:]:
        load.wait()
    x2 = x1_v[...] + mm(sc_v[...], swo[...])
    hn2 = rms_round(x2)
    ff = up.shape[1]
    step = min(512, ff)
    x3 = x2
    for f in range(0, ff, step):
        upper = jnp.maximum(mm(hn2, up[:, f : f + step]), 0.0).astype(BF)
        x3 = x3 + mm(upper, down[f : f + step, :])
    alive = lax.broadcasted_iota(jnp.int32, (n, width), 0) < count
    feat_ref[...] = jnp.where(alive, x3, 0.0)
    hn3 = rms_round(x3)
    b1 = jnp.maximum(mm(hn3, w1[...]), 0.0).astype(BF)
    b2 = jnp.maximum(mm(b1, w2[...]), 0.0).astype(BF)
    z = lax.dot_general(w3[...], b2, (((1,), (1,)), ((), ())), preferred_element_type=F32)
    box = 1.0 / (1.0 + jnp.exp(-z))
    box_ref[...] = jnp.where(lax.broadcasted_iota(jnp.int32, box.shape, 1) < count, box, 0.0)

    each(n_row - 1, lambda i: gather_copy(i).wait_send())


def pin(x):
    return pltpu.with_memory_space_constraint(x, pltpu.HBM)


def local(n_row, *args):
    queries, counts, memory, mem_mask = args[:4]
    weights = args[4:13] + (args[13].T,)
    n, width = queries.shape
    m_dev = memory.shape[0]
    heads = args[14].shape[0]
    keys = n_row * m_dev
    groups = width // LANES
    tm = min(128, n)
    smem = pl.BlockSpec(memory_space=pltpu.SMEM)
    hbm = pl.BlockSpec(memory_space=pltpu.HBM)
    vmem = pl.BlockSpec(memory_space=pltpu.VMEM)
    dma = pltpu.SemaphoreType.DMA
    boxes = weights[-1].shape[0]
    return pl.pallas_call(
        functools.partial(kernel, n_row, width // heads, tm),
        out_shape=(
            jax.ShapeDtypeStruct((n, width), F32),
            jax.ShapeDtypeStruct((boxes, n), F32),
        ),
        in_specs=[hbm, smem, hbm, smem] + [hbm] * 10 + [smem, smem],
        out_specs=(vmem, vmem),
        scratch_shapes=[pltpu.VMEM(queries.shape, BF)]
        + [pltpu.VMEM(w.shape, BF) for w in weights]
        + [
            pltpu.VMEM((n_row, m_dev, width + LANES), BF),
            pltpu.VMEM((2, 8, LANES), jnp.int32),
            pltpu.VMEM((groups, keys, 2 * LANES), BF),
            pltpu.VMEM((groups, keys, 2 * LANES), BF),
            pltpu.VMEM((groups, 2 * n, 2 * LANES), BF),
            pltpu.VMEM((groups, 2 * n, 2 * LANES), BF),
            pltpu.VMEM((n, width), BF),
            pltpu.VMEM((n, width), F32),
            pltpu.VMEM((n, width), BF),
            pltpu.VMEM((n, width), BF),
            pltpu.VMEM((n, width), BF),
            pltpu.VMEM((n, width), BF),
            dma((11,)),
            dma((n_row - 1,)),
            dma((n_row,)),
            dma,
            dma,
            dma((n // tm,)),
            dma((n // tm,)),
            dma,
        ],
        compiler_params=pltpu.CompilerParams(
            collective_id=0, has_side_effects=True, vmem_limit_bytes=52 * 1024 * 1024
        ),
        name="spotter",
    )(pin(queries), counts, pin(memory), mem_mask, *map(pin, weights), *args[14:])


def solution(mesh):
    spread = ("parts", "row", "col")
    return jax.shard_map(
        functools.partial(local, mesh.shape["row"]),
        mesh=mesh,
        in_specs=(P(spread, None), P(spread), P(spread, None), P(spread)) + (P(),) * 12,
        out_specs=(P(spread, None), P(None, spread)),
        check_vma=False,
    )
```

```python
import functools
import math

import jax
import jax.numpy as jnp
from jax import lax
from jax.experimental import pallas as pl
from jax.experimental.pallas import tpu as pltpu
from jax.sharding import PartitionSpec as P

EPS = 1e-06
LANES = 128
BF = jnp.bfloat16
F32 = jnp.float32
MESH = pl.DeviceIdType.MESH
DEAD = 64.0


def rms_round(x):
    return (x * lax.rsqrt(jnp.mean(x * x, axis=-1, keepdims=True) + EPS)).astype(BF)


def mm(a, b):
    return jnp.dot(a, b, preferred_element_type=F32)


def each(n, body):
    if n <= 16:
        for i in range(n):
            body(i)
    else:
        lax.fori_loop(0, n, lambda i, c: (body(i), c)[1], 0)


def scale_row(temp_ref, width, hsize):
    head = lax.broadcasted_iota(jnp.int32, (1, width), 1) // hsize
    row = jnp.zeros((1, width), F32)
    for h in range(width // hsize):
        row = jnp.where(head == h, temp_ref[h], row)
    return row * (math.log2(math.e) / math.sqrt(hsize))


def attend(q, row, ka_ref, va_ref, hsize):
    rows, width = q.shape
    per = LANES // hsize
    qf = q.astype(F32) * row
    hi = qf.astype(BF).astype(F32)
    lo = qf - hi
    head = lax.broadcasted_iota(jnp.int32, (rows, LANES), 1) // hsize
    outs = []
    for g in range(width // LANES):
        lanes = slice(g * LANES, (g + 1) * LANES)
        lhs = jnp.concatenate(
            [
                jnp.concatenate(
                    [jnp.where(head == h, hi[:, lanes], 0.0), jnp.where(head == h, lo[:, lanes], 0.0)],
                    axis=1,
                ).astype(BF)
                for h in range(per)
            ],
            axis=0,
        )
        s = lax.dot_general(lhs, ka_ref[g], (((1,), (1,)), ((), ())), preferred_element_type=F32)
        e = jnp.exp2(s - jnp.max(s, axis=-1, keepdims=True)).astype(BF)
        o = mm(e, va_ref[g])
        num, den = o[:rows, :LANES], o[:rows, LANES:]
        for h in range(1, per):
            part = o[h * rows : (h + 1) * rows]
            num = jnp.where(head == h, part[:, :LANES], num)
            den = jnp.where(head == h, part[:, LANES:], den)
        outs.append(num / den)
    return jnp.concatenate(outs, axis=1)


def put_keys(ka_ref, va_ref, rows, k, v, live, first):
    flags = live.astype(F32).astype(BF)
    for g in range(k.shape[1] // LANES):
        lanes = slice(g * LANES, (g + 1) * LANES)
        kg = jnp.where(live, k[:, lanes], first[:, lanes]).astype(BF)
        ka_ref[g, rows, :LANES] = kg
        ka_ref[g, rows, LANES:] = kg
        va_ref[g, rows, :LANES] = jnp.where(live, v[:, lanes], 0.0).astype(BF)
        va_ref[g, rows, LANES:] = flags


def kernel(
    n_row, hsize, tm,
    q_hbm, cnt_s, mem_hbm, mask_h, wq_h, wkv_h, wo_h, wqkv_h, swo_h, up_h, down_h, w1_h, w2_h, w3_h,
    ct_h, st_h,
    feat_ref, box_ref,
    q_v, wq, wkv, wo, wqkv, swo, up, down, w1, w2, w3,
    mask_s, ct_s, st_s, mem_v, gat, cnt, kac, vac, kas, vas, qc_v, x1_v, hn_v, hn_o, qs_v, sc_v,
    in_sem, gsend, grecv, csend, crecv, hsend, hrecv, msem,
):
    n, width = q_v.shape
    m_dev = mem_hbm.shape[0]
    row = lax.axis_index("row")
    other = 1 - lax.axis_index("col")

    barrier = pltpu.get_barrier_semaphore()

    def greet(i):
        pl.semaphore_signal(
            barrier, inc=1, device_id={"row": lax.rem(row + 1 + i, n_row)}, device_id_type=MESH
        )

    each(n_row - 1, greet)
    pl.semaphore_signal(barrier, inc=1, device_id={"col": other}, device_id_type=MESH)

    small = [
        pltpu.make_async_copy(a, b, msem.at[i])
        for i, (a, b) in enumerate(
            ((mem_hbm, mem_v), (mask_h, mask_s), (ct_h, ct_s), (st_h, st_s))
        )
    ]
    for load in small:
        load.start()
    pairs = (
        (q_hbm, q_v), (wq_h, wq), (wkv_h, wkv), (wo_h, wo), (wqkv_h, wqkv),
        (swo_h, swo), (up_h, up), (down_h, down), (w1_h, w1), (w2_h, w2), (w3_h, w3),
    )
    loads = [pltpu.make_async_copy(a, b, in_sem.at[i]) for i, (a, b) in enumerate(pairs)]
    for load in loads:
        load.start()

    for load in small:
        load.wait()
    slot = lax.broadcasted_iota(jnp.int32, (m_dev, width), 0)
    flags = jnp.zeros((m_dev, width), jnp.int32)
    for i in range(m_dev):
        flags = jnp.where(slot == i, mask_s[i], flags)
    gat[row] = jnp.where(flags > 0, mem_v[...].astype(F32), DEAD).astype(BF)
    count = cnt_s[0]
    cnt[0] = jnp.full((8, LANES), count, jnp.int32)
    loads[0].wait()
    loads[1].wait()
    qc_v[...] = mm(rms_round(q_v[...].astype(F32)), wq[...]).astype(BF)
    pl.semaphore_wait(barrier, n_row)

    def gather_copy(i):
        return pltpu.make_async_remote_copy(
            src_ref=gat.at[row], dst_ref=gat.at[row],
            send_sem=gsend.at[i], recv_sem=grecv.at[row],
            device_id={"row": lax.rem(row + 1 + i, n_row)}, device_id_type=MESH,
        )

    each(n_row - 1, lambda i: gather_copy(i).start())
    count_copy = pltpu.make_async_remote_copy(
        src_ref=cnt.at[0], dst_ref=cnt.at[1], send_sem=csend, recv_sem=crecv,
        device_id={"col": other}, device_id_type=MESH,
    )
    count_copy.start()

    loads[2].wait()

    def arrived(i):
        j = lax.rem(row + 1 + i, n_row)
        pltpu.make_async_remote_copy(
            src_ref=gat.at[j], dst_ref=gat.at[j],
            send_sem=gsend.at[i], recv_sem=grecv.at[j],
            device_id={"row": j}, device_id_type=MESH,
        ).wait_recv()

    each(n_row - 1, arrived)

    keys = n_row * m_dev
    held = gat[...].reshape(keys, width)
    kv = mm(held, wkv[...])
    live = held[:, :LANES].astype(F32) < 0.5 * DEAD
    put_keys(kac, vac, pl.ds(0, keys), kv[:, :width], kv[:, width:], live, kv[0:1, :width])

    cross_row = scale_row(ct_s, width, hsize)
    loads[3].wait()

    def hn_copy(t):
        rows = pl.ds(pl.multiple_of(t * tm, tm), tm)
        return pltpu.make_async_remote_copy(
            src_ref=hn_v.at[rows], dst_ref=hn_o.at[rows],
            send_sem=hsend.at[t], recv_sem=hrecv.at[t],
            device_id={"col": other}, device_id_type=MESH,
        )

    def cross_tile(t, carry):
        rows = pl.ds(pl.multiple_of(t * tm, tm), tm)
        ctx = attend(qc_v[rows, :], cross_row, kac, vac, hsize)
        alive = lax.broadcasted_iota(jnp.int32, (tm, width), 0) + t * tm < count
        ctx = jnp.where(alive, ctx, 0.0).astype(BF)
        x1 = q_v[rows, :].astype(F32) + mm(ctx, wo[...])
        x1_v[rows, :] = x1
        hn_v[rows, :] = rms_round(x1)
        hn_copy(t).start()
        return carry

    lax.fori_loop(0, n // tm, cross_tile, 0)

    loads[4].wait()
    qkv = mm(hn_v[...], wqkv[...])
    qs_v[...] = qkv[:, :width].astype(BF)
    k = qkv[:, width : 2 * width]
    first = k[0:1]
    spot = lax.broadcasted_iota(jnp.int32, (n, LANES), 0)
    put_keys(kas, vas, pl.ds(0, n), k, qkv[:, 2 * width :], spot < count, first)
    count_copy.wait()
    each(n // tm, lambda t: hn_copy(t).wait())
    kv_o = mm(hn_o[...], wqkv[:, width:])
    put_keys(kas, vas, pl.ds(n, n), kv_o[:, :width], kv_o[:, width:], spot < cnt[1, 0:1, :], first)

    self_row = scale_row(st_s, width, hsize)

    def self_tile(t, carry):
        rows = pl.ds(pl.multiple_of(t * tm, tm), tm)
        sctx = attend(qs_v[rows, :], self_row, kas, vas, hsize)
        alive = lax.broadcasted_iota(jnp.int32, (tm, width), 0) + t * tm < count
        sc_v[rows, :] = jnp.where(alive, sctx, 0.0).astype(BF)
        return carry

    lax.fori_loop(0, n // tm, self_tile, 0)

    for load in loads[5:]:
        load.wait()
    x2 = x1_v[...] + mm(sc_v[...], swo[...])
    hn2 = rms_round(x2)
    ff = up.shape[1]
    step = min(512, ff)
    x3 = x2
    for f in range(0, ff, step):
        upper = jnp.maximum(mm(hn2, up[:, f : f + step]), 0.0).astype(BF)
        x3 = x3 + mm(upper, down[f : f + step, :])
    alive = lax.broadcasted_iota(jnp.int32, (n, width), 0) < count
    feat_ref[...] = jnp.where(alive, x3, 0.0)
    hn3 = rms_round(x3)
    b1 = jnp.maximum(mm(hn3, w1[...]), 0.0).astype(BF)
    b2 = jnp.maximum(mm(b1, w2[...]), 0.0).astype(BF)
    z = lax.dot_general(w3[...], b2, (((1,), (1,)), ((), ())), preferred_element_type=F32)
    box = 1.0 / (1.0 + jnp.exp(-z))
    box_ref[...] = jnp.where(lax.broadcasted_iota(jnp.int32, box.shape, 1) < count, box, 0.0)

    each(n_row - 1, lambda i: gather_copy(i).wait_send())


def pin(x):
    return pltpu.with_memory_space_constraint(x, pltpu.HBM)


def local(n_row, *args):
    queries, counts, memory, mem_mask = args[:4]
    weights = args[4:13] + (args[13].T,)
    n, width = queries.shape
    m_dev = memory.shape[0]
    heads = args[14].shape[0]
    keys = n_row * m_dev
    groups = width // LANES
    tm = min(256, n)
    hbm = pl.BlockSpec(memory_space=pltpu.HBM)
    vmem = pl.BlockSpec(memory_space=pltpu.VMEM)
    dma = pltpu.SemaphoreType.DMA
    boxes = weights[-1].shape[0]
    return pl.pallas_call(
        functools.partial(kernel, n_row, width // heads, tm),
        out_shape=(
            jax.ShapeDtypeStruct((n, width), F32),
            jax.ShapeDtypeStruct((boxes, n), F32),
        ),
        in_specs=[hbm, pl.BlockSpec(memory_space=pltpu.SMEM)] + [hbm] * 14,
        out_specs=(vmem, vmem),
        scratch_shapes=[pltpu.VMEM(queries.shape, BF)]
        + [pltpu.VMEM(w.shape, BF) for w in weights]
        + [
            pltpu.SMEM(mem_mask.shape, jnp.int32),
            pltpu.SMEM((heads,), F32),
            pltpu.SMEM((heads,), F32),
            pltpu.VMEM(memory.shape, BF),
            pltpu.VMEM((n_row, m_dev, width), BF),
            pltpu.VMEM((2, 8, LANES), jnp.int32),
            pltpu.VMEM((groups, keys, 2 * LANES), BF),
            pltpu.VMEM((groups, keys, 2 * LANES), BF),
            pltpu.VMEM((groups, 2 * n, 2 * LANES), BF),
            pltpu.VMEM((groups, 2 * n, 2 * LANES), BF),
            pltpu.VMEM((n, width), BF),
            pltpu.VMEM((n, width), F32),
            pltpu.VMEM((n, width), BF),
            pltpu.VMEM((n, width), BF),
            pltpu.VMEM((n, width), BF),
            pltpu.VMEM((n, width), BF),
            dma((11,)),
            dma((n_row - 1,)),
            dma((n_row,)),
            dma,
            dma,
            dma((n // tm,)),
            dma((n // tm,)),
            dma((4,)),
        ],
        compiler_params=pltpu.CompilerParams(
            collective_id=0, has_side_effects=True, vmem_limit_bytes=52 * 1024 * 1024
        ),
        name="spotter",
    )(pin(queries), counts, *map(pin, args[2:4] + weights + args[14:]))


def solution(mesh):
    spread = ("parts", "row", "col")
    return jax.shard_map(
        functools.partial(local, mesh.shape["row"]),
        mesh=mesh,
        in_specs=(P(spread, None), P(spread), P(spread, None), P(spread)) + (P(),) * 12,
        out_specs=(P(spread, None), P(None, spread)),
        check_vma=False,
    )
```

```python
import functools
import math

import jax
import jax.numpy as jnp
from jax import lax
from jax.experimental import pallas as pl
from jax.experimental.pallas import tpu as pltpu
from jax.sharding import PartitionSpec as P

EPS = 1e-06
LANES = 128
BF = jnp.bfloat16
F32 = jnp.float32
MESH = pl.DeviceIdType.MESH
DEAD = 64.0


def rms_round(x):
    return (x * lax.rsqrt(jnp.mean(x * x, axis=-1, keepdims=True) + EPS)).astype(BF)


def mm(a, b):
    return jnp.dot(a, b, preferred_element_type=F32)


def each(n, body):
    if n <= 16:
        for i in range(n):
            body(i)
    else:
        lax.fori_loop(0, n, lambda i, c: (body(i), c)[1], 0)


def scale_row(temp_ref, width, hsize):
    head = lax.broadcasted_iota(jnp.int32, (1, width), 1) // hsize
    row = jnp.zeros((1, width), F32)
    for h in range(width // hsize):
        row = jnp.where(head == h, temp_ref[h], row)
    return row * (math.log2(math.e) / math.sqrt(hsize))


def attend(q, row, ka_ref, va_ref, keys, hsize):
    rows, width = q.shape
    per = LANES // hsize
    qf = q.astype(F32) * row
    hi = qf.astype(BF).astype(F32)
    lo = qf - hi
    head = lax.broadcasted_iota(jnp.int32, (rows, LANES), 1) // hsize
    outs = []
    for g in range(width // LANES):
        lanes = slice(g * LANES, (g + 1) * LANES)
        lhs = jnp.concatenate(
            [
                jnp.concatenate(
                    [jnp.where(head == h, hi[:, lanes], 0.0), jnp.where(head == h, lo[:, lanes], 0.0)],
                    axis=1,
                ).astype(BF)
                for h in range(per)
            ],
            axis=0,
        )
        s = lax.dot_general(lhs, ka_ref[g, :keys], (((1,), (1,)), ((), ())), preferred_element_type=F32)
        e = jnp.exp2(s - jnp.max(s, axis=-1, keepdims=True)).astype(BF)
        o = mm(e, va_ref[g, :keys])
        num, den = o[:rows, :LANES], o[:rows, LANES:]
        for h in range(1, per):
            part = o[h * rows : (h + 1) * rows]
            num = jnp.where(head == h, part[:, :LANES], num)
            den = jnp.where(head == h, part[:, LANES:], den)
        outs.append(num / den)
    return jnp.concatenate(outs, axis=1)


def put_keys(ka_ref, va_ref, rows, k, v, live, first):
    flags = live.astype(F32).astype(BF)
    for g in range(k.shape[1] // LANES):
        lanes = slice(g * LANES, (g + 1) * LANES)
        kg = jnp.where(live, k[:, lanes], first[:, lanes]).astype(BF)
        ka_ref[g, rows, :LANES] = kg
        ka_ref[g, rows, LANES:] = kg
        va_ref[g, rows, :LANES] = jnp.where(live, v[:, lanes], 0.0).astype(BF)
        va_ref[g, rows, LANES:] = flags


def mixer(
    n_row, hsize, tm,
    q_hbm, cnt_s, mem_hbm, mask_h, wq_h, wkv_h, wo_h, wqkv_h, swo_h, up_h, down_h, w1_h, w2_h, w3_h, ct_h, st_h,
    x1_v, qs_v, kas, vas, cnt, self_row, swo, up, down, w1, w2, w3,
    q_v, wq, wkv, wo, wqkv,
    mask_s, ct_s, st_s, mem_v, gat, kac, vac, qc_v, hn_v, hn_o,
    in_sem, gsend, grecv, csend, crecv, hsend, hrecv, msem,
):
    n, width = q_v.shape
    m_dev = mem_hbm.shape[0]
    row = lax.axis_index("row")
    other = 1 - lax.axis_index("col")

    barrier = pltpu.get_barrier_semaphore()

    def greet(i):
        pl.semaphore_signal(
            barrier, inc=1, device_id={"row": lax.rem(row + 1 + i, n_row)}, device_id_type=MESH
        )

    each(n_row - 1, greet)
    pl.semaphore_signal(barrier, inc=1, device_id={"col": other}, device_id_type=MESH)

    small = [
        pltpu.make_async_copy(a, b, msem.at[i])
        for i, (a, b) in enumerate(
            ((mem_hbm, mem_v), (mask_h, mask_s), (ct_h, ct_s), (st_h, st_s))
        )
    ]
    for load in small:
        load.start()
    pairs = (
        (q_hbm, q_v), (wq_h, wq), (wkv_h, wkv), (wo_h, wo), (wqkv_h, wqkv),
        (swo_h, swo), (up_h, up), (down_h, down), (w1_h, w1), (w2_h, w2), (w3_h, w3),
    )
    loads = [pltpu.make_async_copy(a, b, in_sem.at[i]) for i, (a, b) in enumerate(pairs)]
    for load in loads:
        load.start()

    for load in small:
        load.wait()
    slot = lax.broadcasted_iota(jnp.int32, (m_dev, width), 0)
    flags = jnp.zeros((m_dev, width), jnp.int32)
    for i in range(m_dev):
        flags = jnp.where(slot == i, mask_s[i], flags)
    gat[row] = jnp.where(flags > 0, mem_v[...].astype(F32), DEAD).astype(BF)
    count = cnt_s[0]
    cnt[0] = jnp.full((8, LANES), count, jnp.int32)
    loads[0].wait()
    loads[1].wait()
    qc_v[...] = mm(rms_round(q_v[...].astype(F32)), wq[...]).astype(BF)
    self_row[...] = scale_row(st_s, width, hsize)
    pl.semaphore_wait(barrier, n_row)

    def gather_copy(i):
        return pltpu.make_async_remote_copy(
            src_ref=gat.at[row], dst_ref=gat.at[row],
            send_sem=gsend.at[i], recv_sem=grecv.at[row],
            device_id={"row": lax.rem(row + 1 + i, n_row)}, device_id_type=MESH,
        )

    each(n_row - 1, lambda i: gather_copy(i).start())
    count_copy = pltpu.make_async_remote_copy(
        src_ref=cnt.at[0], dst_ref=cnt.at[1], send_sem=csend, recv_sem=crecv,
        device_id={"col": other}, device_id_type=MESH,
    )
    count_copy.start()

    loads[2].wait()

    def arrived(i):
        j = lax.rem(row + 1 + i, n_row)
        pltpu.make_async_remote_copy(
            src_ref=gat.at[j], dst_ref=gat.at[j],
            send_sem=gsend.at[i], recv_sem=grecv.at[j],
            device_id={"row": j}, device_id_type=MESH,
        ).wait_recv()

    each(n_row - 1, arrived)

    keys = n_row * m_dev
    held = gat[...].reshape(keys, width)
    kv = mm(held, wkv[...])
    live = held[:, :LANES].astype(F32) < 0.5 * DEAD
    put_keys(kac, vac, pl.ds(0, keys), kv[:, :width], kv[:, width:], live, kv[0:1, :width])

    cross_row = scale_row(ct_s, width, hsize)
    loads[3].wait()

    def hn_copy(t):
        rows = pl.ds(pl.multiple_of(t * tm, tm), tm)
        return pltpu.make_async_remote_copy(
            src_ref=hn_v.at[rows], dst_ref=hn_o.at[rows],
            send_sem=hsend.at[t], recv_sem=hrecv.at[t],
            device_id={"col": other}, device_id_type=MESH,
        )

    def cross_tile(t, carry):
        rows = pl.ds(pl.multiple_of(t * tm, tm), tm)
        ctx = attend(qc_v[rows, :], cross_row, kac, vac, keys, hsize)
        alive = lax.broadcasted_iota(jnp.int32, (tm, width), 0) + t * tm < count
        ctx = jnp.where(alive, ctx, 0.0).astype(BF)
        x1 = q_v[rows, :].astype(F32) + mm(ctx, wo[...])
        x1_v[rows, :] = x1
        hn_v[rows, :] = rms_round(x1)
        hn_copy(t).start()
        return carry

    lax.fori_loop(0, n // tm, cross_tile, 0)

    loads[4].wait()
    qkv = mm(hn_v[...], wqkv[...])
    qs_v[...] = qkv[:, :width].astype(BF)
    k = qkv[:, width : 2 * width]
    first = k[0:1]
    spot = lax.broadcasted_iota(jnp.int32, (n, LANES), 0)
    put_keys(kas, vas, pl.ds(0, n), k, qkv[:, 2 * width :], spot < count, first)
    count_copy.wait()
    each(n // tm, lambda t: hn_copy(t).wait())
    kv_o = mm(hn_o[...], wqkv[:, width:])
    put_keys(kas, vas, pl.ds(n, n), kv_o[:, :width], kv_o[:, width:], spot < cnt[1, 0:1, :], first)

    for load in loads[5:]:
        load.wait()
    each(n_row - 1, lambda i: gather_copy(i).wait_send())


def reader(
    hsize, tm,
    x1_v, qs_v, kas, vas, cnt, self_row, swo, up, down, w1, w2, w3,
    feat_ref, box_ref,
    sc_v, out_v, box_v, sems,
):
    n, width = x1_v.shape
    count = jnp.max(cnt[0])
    theirs = jnp.max(cnt[1])
    sc_v[...] = jnp.zeros_like(sc_v)
    unit = min(LANES, n)
    for i in range(n // unit):

        @pl.when((theirs - 1) // unit == i)
        def _():
            def self_tile(t, carry):
                rows = pl.ds(pl.multiple_of(t * tm, tm), tm)
                sctx = attend(qs_v[rows, :], self_row[...], kas, vas, n + (i + 1) * unit, hsize)
                alive = lax.broadcasted_iota(jnp.int32, (tm, width), 0) + t * tm < count
                sc_v[rows, :] = jnp.where(alive, sctx, 0.0).astype(BF)
                return carry

            lax.fori_loop(0, (count + tm - 1) // tm, self_tile, 0)

    x2 = x1_v[...] + mm(sc_v[...], swo[...])
    hn2 = rms_round(x2)
    ff = up.shape[1]
    step = min(512, ff)
    x3 = x2
    for f in range(0, ff, step):
        upper = jnp.maximum(mm(hn2, up[:, f : f + step]), 0.0).astype(BF)
        x3 = x3 + mm(upper, down[f : f + step, :])
    alive = lax.broadcasted_iota(jnp.int32, (n, width), 0) < count
    out_v[...] = jnp.where(alive, x3, 0.0)
    put = pltpu.make_async_copy(out_v, feat_ref, sems.at[0])
    put.start()
    hn3 = rms_round(x3)
    b1 = jnp.maximum(mm(hn3, w1[...]), 0.0).astype(BF)
    b2 = jnp.maximum(mm(b1, w2[...]), 0.0).astype(BF)
    z = lax.dot_general(w3[...], b2, (((1,), (1,)), ((), ())), preferred_element_type=F32)
    box = 1.0 / (1.0 + jnp.exp(-z))
    box_v[...] = jnp.where(lax.broadcasted_iota(jnp.int32, box.shape, 1) < count, box, 0.0)
    put_box = pltpu.make_async_copy(box_v, box_ref, sems.at[1])
    put_box.start()
    put.wait()
    put_box.wait()


def pin(x):
    return pltpu.with_memory_space_constraint(x, pltpu.HBM)


def local(n_row, *args):
    queries, counts, memory, mem_mask = args[:4]
    weights = args[4:13] + (args[13].T,)
    n, width = queries.shape
    m_dev = memory.shape[0]
    heads = args[14].shape[0]
    keys = n_row * m_dev
    groups = width // LANES
    tm = min(256, n)
    hbm = pl.BlockSpec(memory_space=pltpu.HBM)
    smem = pl.BlockSpec(memory_space=pltpu.SMEM)
    vmem = pl.BlockSpec(memory_space=pltpu.VMEM)
    dma = pltpu.SemaphoreType.DMA
    boxes = weights[-1].shape[0]
    like = jax.ShapeDtypeStruct
    held = pl.pallas_call(
        functools.partial(mixer, n_row, width // heads, tm),
        out_shape=(
            like((n, width), F32),
            like((n, width), BF),
            like((groups, 2 * n, 2 * LANES), BF),
            like((groups, 2 * n, 2 * LANES), BF),
            like((2, 8, LANES), jnp.int32),
            like((1, width), F32),
        )
        + tuple(like(w.shape, BF) for w in weights[4:]),
        in_specs=[hbm, smem] + [hbm] * 14,
        out_specs=(vmem,) * (6 + len(weights[4:])),
        scratch_shapes=[pltpu.VMEM(queries.shape, BF)]
        + [pltpu.VMEM(w.shape, BF) for w in weights[:4]]
        + [
            pltpu.SMEM(mem_mask.shape, jnp.int32),
            pltpu.SMEM((heads,), F32),
            pltpu.SMEM((heads,), F32),
            pltpu.VMEM(memory.shape, BF),
            pltpu.VMEM((n_row, m_dev, width), BF),
            pltpu.VMEM((groups, keys, 2 * LANES), BF),
            pltpu.VMEM((groups, keys, 2 * LANES), BF),
            pltpu.VMEM((n, width), BF),
            pltpu.VMEM((n, width), BF),
            pltpu.VMEM((n, width), BF),
            dma((11,)),
            dma((n_row - 1,)),
            dma((n_row,)),
            dma,
            dma,
            dma((n // tm,)),
            dma((n // tm,)),
            dma((4,)),
        ],
        compiler_params=pltpu.CompilerParams(
            collective_id=0, has_side_effects=True, vmem_limit_bytes=32 * 1024 * 1024
        ),
        name="mixer",
    )(pin(queries), counts, *map(pin, args[2:4] + weights + args[14:]))
    return pl.pallas_call(
        functools.partial(reader, width // heads, tm),
        out_shape=(like((n, width), F32), like((boxes, n), F32)),
        in_specs=[vmem] * 12,
        out_specs=(hbm, hbm),
        scratch_shapes=[
            pltpu.VMEM((n, width), BF),
            pltpu.VMEM((n, width), F32),
            pltpu.VMEM((boxes, n), F32),
            dma((2,)),
        ],
        compiler_params=pltpu.CompilerParams(vmem_limit_bytes=32 * 1024 * 1024),
        name="reader",
    )(*held)


def solution(mesh):
    spread = ("parts", "row", "col")
    return jax.shard_map(
        functools.partial(local, mesh.shape["row"]),
        mesh=mesh,
        in_specs=(P(spread, None), P(spread), P(spread, None), P(spread)) + (P(),) * 12,
        out_specs=(P(spread, None), P(None, spread)),
        check_vma=False,
    )
```

```python
import functools
import math

import jax
import jax.numpy as jnp
from jax import lax
from jax.experimental import pallas as pl
from jax.experimental.pallas import tpu as pltpu
from jax.sharding import PartitionSpec as P

EPS = 1e-06
LANES = 128
BF = jnp.bfloat16
F32 = jnp.float32
MESH = pl.DeviceIdType.MESH
DEAD = 64.0


def rms_round(x):
    return (x * lax.rsqrt(jnp.mean(x * x, axis=-1, keepdims=True) + EPS)).astype(BF)


def mm(a, b):
    return jnp.dot(a, b, preferred_element_type=F32)


def each(n, body):
    if n <= 16:
        for i in range(n):
            body(i)
    else:
        lax.fori_loop(0, n, lambda i, c: (body(i), c)[1], 0)


def scale_row(temp_ref, width, hsize):
    head = lax.broadcasted_iota(jnp.int32, (1, width), 1) // hsize
    row = jnp.zeros((1, width), F32)
    for h in range(width // hsize):
        row = jnp.where(head == h, temp_ref[h], row)
    return row * (math.log2(math.e) / math.sqrt(hsize))


def attend(q, row, ka_ref, va_ref, keys, hsize):
    rows, width = q.shape
    per = LANES // hsize
    qf = q.astype(F32) * row
    hi = qf.astype(BF).astype(F32)
    lo = qf - hi
    head = lax.broadcasted_iota(jnp.int32, (rows, LANES), 1) // hsize
    outs = []
    for g in range(width // LANES):
        lanes = slice(g * LANES, (g + 1) * LANES)
        lhs = jnp.concatenate(
            [
                jnp.concatenate(
                    [jnp.where(head == h, hi[:, lanes], 0.0), jnp.where(head == h, lo[:, lanes], 0.0)],
                    axis=1,
                ).astype(BF)
                for h in range(per)
            ],
            axis=0,
        )
        s = lax.dot_general(lhs, ka_ref[g, :keys], (((1,), (1,)), ((), ())), preferred_element_type=F32)
        e = jnp.exp2(s - jnp.max(s, axis=-1, keepdims=True)).astype(BF)
        o = mm(e, va_ref[g, :keys])
        num, den = o[:rows, :LANES], o[:rows, LANES:]
        for h in range(1, per):
            part = o[h * rows : (h + 1) * rows]
            num = jnp.where(head == h, part[:, :LANES], num)
            den = jnp.where(head == h, part[:, LANES:], den)
        outs.append(num / den)
    return jnp.concatenate(outs, axis=1)


def put_keys(ka_ref, va_ref, rows, k, v, live, first):
    flags = live.astype(F32).astype(BF)
    for g in range(k.shape[1] // LANES):
        lanes = slice(g * LANES, (g + 1) * LANES)
        kg = jnp.where(live, k[:, lanes], first[:, lanes]).astype(BF)
        ka_ref[g, rows, :LANES] = kg
        ka_ref[g, rows, LANES:] = kg
        va_ref[g, rows, :LANES] = jnp.where(live, v[:, lanes], 0.0).astype(BF)
        va_ref[g, rows, LANES:] = flags


def mixer(
    n_row, hsize, tm,
    q_hbm, cnt_s, mem_hbm, mask_h, wq_h, wkv_h, wo_h, wqkv_h, swo_h, up_h, down_h, w1_h, w2_h, w3_h, ct_h, st_h,
    x1_v, qs_v, kas, vas, cnt, self_row, swo, up, down, w1, w2, w3,
    q_v, wq, wkv, wo, wqkv,
    mask_s, ct_s, st_s, mem_v, gat, kac, vac, qc_v, hn_v, hn_o,
    in_sem, gsend, grecv, csend, crecv, hsend, hrecv, msem,
):
    n, width = q_v.shape
    m_dev = mem_hbm.shape[0]
    row = lax.axis_index("row")
    other = 1 - lax.axis_index("col")

    barrier = pltpu.get_barrier_semaphore()

    def greet(i):
        pl.semaphore_signal(
            barrier, inc=1, device_id={"row": lax.rem(row + 1 + i, n_row)}, device_id_type=MESH
        )

    each(n_row - 1, greet)
    pl.semaphore_signal(barrier, inc=1, device_id={"col": other}, device_id_type=MESH)

    small = [
        pltpu.make_async_copy(a, b, msem.at[i])
        for i, (a, b) in enumerate(
            ((mem_hbm, mem_v), (mask_h, mask_s), (ct_h, ct_s), (st_h, st_s))
        )
    ]
    for load in small:
        load.start()
    pairs = (
        (q_hbm, q_v), (wq_h, wq), (wkv_h, wkv), (wo_h, wo), (wqkv_h, wqkv),
        (swo_h, swo), (up_h, up), (down_h, down), (w1_h, w1), (w2_h, w2), (w3_h, w3),
    )
    loads = [pltpu.make_async_copy(a, b, in_sem.at[i]) for i, (a, b) in enumerate(pairs)]
    for load in loads:
        load.start()

    for load in small:
        load.wait()
    slot = lax.broadcasted_iota(jnp.int32, (m_dev, width), 0)
    flags = jnp.zeros((m_dev, width), jnp.int32)
    for i in range(m_dev):
        flags = jnp.where(slot == i, mask_s[i], flags)
    gat[row] = jnp.where(flags > 0, mem_v[...].astype(F32), DEAD).astype(BF)
    count = cnt_s[0]
    cnt[0] = jnp.full((8, LANES), count, jnp.int32)
    loads[0].wait()
    loads[1].wait()
    qc_v[...] = mm(rms_round(q_v[...].astype(F32)), wq[...]).astype(BF)
    self_row[...] = scale_row(st_s, width, hsize)
    pl.semaphore_wait(barrier, n_row)

    def gather_copy(i):
        return pltpu.make_async_remote_copy(
            src_ref=gat.at[row], dst_ref=gat.at[row],
            send_sem=gsend.at[i], recv_sem=grecv.at[row],
            device_id={"row": lax.rem(row + 1 + i, n_row)}, device_id_type=MESH,
        )

    each(n_row - 1, lambda i: gather_copy(i).start())
    count_copy = pltpu.make_async_remote_copy(
        src_ref=cnt.at[0], dst_ref=cnt.at[1], send_sem=csend, recv_sem=crecv,
        device_id={"col": other}, device_id_type=MESH,
    )
    count_copy.start()

    loads[2].wait()

    def arrived(i):
        j = lax.rem(row + 1 + i, n_row)
        pltpu.make_async_remote_copy(
            src_ref=gat.at[j], dst_ref=gat.at[j],
            send_sem=gsend.at[i], recv_sem=grecv.at[j],
            device_id={"row": j}, device_id_type=MESH,
        ).wait_recv()

    each(n_row - 1, arrived)

    keys = n_row * m_dev
    held = gat[...].reshape(keys, width)
    kv = mm(held, wkv[...])
    live = held[:, :LANES].astype(F32) < 0.5 * DEAD
    put_keys(kac, vac, pl.ds(0, keys), kv[:, :width], kv[:, width:], live, kv[0:1, :width])

    cross_row = scale_row(ct_s, width, hsize)
    loads[3].wait()

    def hn_copy(t):
        rows = pl.ds(pl.multiple_of(t * tm, tm), tm)
        return pltpu.make_async_remote_copy(
            src_ref=hn_v.at[rows], dst_ref=hn_o.at[rows],
            send_sem=hsend.at[t], recv_sem=hrecv.at[t],
            device_id={"col": other}, device_id_type=MESH,
        )

    def cross_tile(t, carry):
        rows = pl.ds(pl.multiple_of(t * tm, tm), tm)
        ctx = attend(qc_v[rows, :], cross_row, kac, vac, keys, hsize)
        alive = lax.broadcasted_iota(jnp.int32, (tm, width), 0) + t * tm < count
        ctx = jnp.where(alive, ctx, 0.0).astype(BF)
        x1 = q_v[rows, :].astype(F32) + mm(ctx, wo[...])
        x1_v[rows, :] = x1
        hn_v[rows, :] = rms_round(x1)
        hn_copy(t).start()
        return carry

    lax.fori_loop(0, n // tm, cross_tile, 0)

    loads[4].wait()
    qkv = mm(hn_v[...], wqkv[...])
    qs_v[...] = qkv[:, :width].astype(BF)
    k = qkv[:, width : 2 * width]
    first = k[0:1]
    spot = lax.broadcasted_iota(jnp.int32, (n, LANES), 0)
    put_keys(kas, vas, pl.ds(0, n), k, qkv[:, 2 * width :], spot < count, first)
    count_copy.wait()
    each(n // tm, lambda t: hn_copy(t).wait())
    kv_o = mm(hn_o[...], wqkv[:, width:])
    put_keys(kas, vas, pl.ds(n, n), kv_o[:, :width], kv_o[:, width:], spot < cnt[1, 0:1, :], first)

    for load in loads[5:]:
        load.wait()
    each(n_row - 1, lambda i: gather_copy(i).wait_send())


def reader(
    hsize, tm,
    x1_v, qs_v, kas, vas, cnt, self_row, swo, up, down, w1, w2, w3,
    feat_ref, box_ref,
    sc_v, out_v, box_v, sems,
):
    n, width = x1_v.shape
    count = jnp.max(cnt[0])
    theirs = jnp.max(cnt[1])
    sc_v[...] = jnp.zeros_like(sc_v)
    unit = min(LANES, n)
    for i in range(n // unit):

        @pl.when((theirs - 1) // unit == i)
        def _():
            def self_tile(t, carry):
                rows = pl.ds(pl.multiple_of(t * tm, tm), tm)
                sctx = attend(qs_v[rows, :], self_row[...], kas, vas, n + (i + 1) * unit, hsize)
                alive = lax.broadcasted_iota(jnp.int32, (tm, width), 0) + t * tm < count
                sc_v[rows, :] = jnp.where(alive, sctx, 0.0).astype(BF)
                return carry

            lax.fori_loop(0, (count + tm - 1) // tm, self_tile, 0)

    x2 = x1_v[...] + mm(sc_v[...], swo[...])
    hn2 = rms_round(x2)
    ff = up.shape[1]
    step = min(512, ff)
    x3 = x2
    for f in range(0, ff, step):
        upper = jnp.maximum(mm(hn2, up[:, f : f + step]), 0.0).astype(BF)
        x3 = x3 + mm(upper, down[f : f + step, :])
    alive = lax.broadcasted_iota(jnp.int32, (n, width), 0) < count
    out_v[...] = jnp.where(alive, x3, 0.0)
    put = pltpu.make_async_copy(out_v, feat_ref, sems.at[0])
    put.start()
    hn3 = rms_round(x3)
    b1 = jnp.maximum(mm(hn3, w1[...]), 0.0).astype(BF)
    b2 = jnp.maximum(mm(b1, w2[...]), 0.0).astype(BF)
    z = lax.dot_general(w3[...], b2, (((1,), (1,)), ((), ())), preferred_element_type=F32)
    box = 1.0 / (1.0 + jnp.exp(-z))
    box_v[...] = jnp.where(lax.broadcasted_iota(jnp.int32, box.shape, 1) < count, box, 0.0)
    put_box = pltpu.make_async_copy(box_v, box_ref, sems.at[1])
    put_box.start()
    put.wait()
    put_box.wait()


def pin(x):
    return pltpu.with_memory_space_constraint(x, pltpu.HBM)


def local(n_row, *args):
    queries, counts, memory, mem_mask = args[:4]
    weights = args[4:13] + (args[13].T,)
    n, width = queries.shape
    m_dev = memory.shape[0]
    heads = args[14].shape[0]
    keys = n_row * m_dev
    groups = width // LANES
    tm = min(256, n)
    hbm = pl.BlockSpec(memory_space=pltpu.HBM)
    smem = pl.BlockSpec(memory_space=pltpu.SMEM)
    vmem = pl.BlockSpec(memory_space=pltpu.VMEM)
    dma = pltpu.SemaphoreType.DMA
    boxes = weights[-1].shape[0]
    like = jax.ShapeDtypeStruct
    held = pl.pallas_call(
        functools.partial(mixer, n_row, width // heads, tm),
        out_shape=(
            like((n, width), F32),
            like((n, width), BF),
            like((groups, 2 * n, 2 * LANES), BF),
            like((groups, 2 * n, 2 * LANES), BF),
            like((2, 8, LANES), jnp.int32),
            like((1, width), F32),
        )
        + tuple(like(w.shape, BF) for w in weights[4:]),
        in_specs=[hbm, smem] + [hbm] * 14,
        out_specs=(vmem,) * (6 + len(weights[4:])),
        scratch_shapes=[pltpu.VMEM(queries.shape, BF)]
        + [pltpu.VMEM(w.shape, BF) for w in weights[:4]]
        + [
            pltpu.SMEM(mem_mask.shape, jnp.int32),
            pltpu.SMEM((heads,), F32),
            pltpu.SMEM((heads,), F32),
            pltpu.VMEM(memory.shape, BF),
            pltpu.VMEM((n_row, m_dev, width), BF),
            pltpu.VMEM((groups, keys, 2 * LANES), BF),
            pltpu.VMEM((groups, keys, 2 * LANES), BF),
            pltpu.VMEM((n, width), BF),
            pltpu.VMEM((n, width), BF),
            pltpu.VMEM((n, width), BF),
            dma((11,)),
            dma((n_row - 1,)),
            dma((n_row,)),
            dma,
            dma,
            dma((n // tm,)),
            dma((n // tm,)),
            dma((4,)),
        ],
        compiler_params=pltpu.CompilerParams(
            collective_id=0, has_side_effects=True, vmem_limit_bytes=32 * 1024 * 1024
        ),
        name="mixer",
    )(pin(queries), counts, *map(pin, args[2:4] + weights + args[14:]))
    return pl.pallas_call(
        functools.partial(reader, width // heads, min(512, n)),
        out_shape=(like((n, width), F32), like((boxes, n), F32)),
        in_specs=[vmem] * 12,
        out_specs=(hbm, hbm),
        scratch_shapes=[
            pltpu.VMEM((n, width), BF),
            pltpu.VMEM((n, width), F32),
            pltpu.VMEM((boxes, n), F32),
            dma((2,)),
        ],
        compiler_params=pltpu.CompilerParams(vmem_limit_bytes=32 * 1024 * 1024),
        name="reader",
    )(*held)


def solution(mesh):
    spread = ("parts", "row", "col")
    return jax.shard_map(
        functools.partial(local, mesh.shape["row"]),
        mesh=mesh,
        in_specs=(P(spread, None), P(spread), P(spread, None), P(spread)) + (P(),) * 12,
        out_specs=(P(spread, None), P(None, spread)),
        check_vma=False,
    )
```
